512 devices in a mesh: dp: 4 (over z_lo, core), ctx: 32 (over z_hi, y), tp: 4 (over x).
Axes of the slice: x: 4, y: 8, z: 8 (z_hi: 4, z_lo: 2; z = z_hi * 2 + z_lo), core: 2. Of those that a mesh axis runs over, the one named last changes fastest.
Arguments:
- queries: bfloat16 [16384, 4096], P(('dp', 'ctx'), 'tp'), parts along dimension 0, may hold values from -40 to 40
- keys: bfloat16 [16384, 4096], P(('dp', 'ctx'), 'tp'), parts along dimension 0, may hold values from -40 to 40
- values: bfloat16 [16384, 4096], P(('dp', 'ctx'), 'tp'), parts along dimension 0, may hold values from -6 to 6
- query_gain: float32 [4096], P('tp'), may hold values from 0.1 to 1.9
- key_gain: float32 [4096], P('tp'), may hold values from 0.1 to 1.9
- block_mask: int32 [32, 32], P('ctx'), may hold values from 0 to 1, as said below
Outputs:
- attended: bfloat16 [16384, 4096], P(('dp', 'ctx'), 'tp'), parts along dimension 0
The draws below stay inside these ranges and needn't reach their ends.
There are 4 independent parts, one for each index of `dp`. The reference program is written for one: setup_inputs(seed, part) draws one part's arguments, and reference() takes and returns one part's arrays. A program takes and returns all parts, laid end to end along the dimension named above; an argument that names none is the same for every part. Nothing has to cross between parts.
Inputs may be any that keep to these rules, and one draw needn't show every extreme that they name: block_mask[i, i] is 1 for every i, and block_mask[i, j] is 0 unless |i - j| is a power of two.
All inputs are finite; a program needn't handle non-finite values.
Results may differ from the reference program's by a relative error of at most 0.011.
Values may be sent and summed in bfloat16 or wider, within the bound.
No kernel may reach another device: no remote copies, remote signals or barrier semaphores. Data moves between devices by JAX's collectives and lax.ppermute only.
A program may use at most 128 MiB of HBM per device.

```python
import jax
import jax.numpy as jnp
from jax import lax

HEADS = 32
HD = 128
BLOCK = 128
TOKENS = 4096
NB = 32
CH = 4096


def joint_rows(base_key):
    head_pos = jnp.arange(HEADS).astype(jnp.float32) / max(HEADS - 1, 1)
    column_scale = 3.0 ** head_pos

    def base_rows(index_tag):
        noise = jnp.clip(jax.random.normal(jax.random.fold_in(base_key, index_tag), (TOKENS, HEADS, HD), jnp.float32), -4.0, 4.0)
        noise = noise * column_scale[None, :, None]
        return noise
    query_rows = base_rows(1)
    key_rows = base_rows(2)
    query_rows = jnp.clip(query_rows, -40.0, 40.0).reshape(TOKENS, HEADS * HD)
    key_rows = jnp.clip(key_rows, -40.0, 40.0).reshape(TOKENS, HEADS * HD)
    return (query_rows, key_rows)


def draw_queries(key, part):
    return joint_rows(jax.random.fold_in(key, 77))[0].astype(jnp.bfloat16)


def draw_keys(key, part):
    return joint_rows(jax.random.fold_in(key, 77))[1].astype(jnp.bfloat16)


def draw_block_mask(key, part):
    row_ids = jnp.arange(NB)[:, None]
    col_ids = jnp.arange(NB)[None, :]
    distance = jnp.abs(row_ids - col_ids)
    power_two = (distance > 0) & (distance & distance - 1 == 0)
    coin_bits = jax.random.randint(key, (NB, NB), 0, 2)
    return jnp.where(distance == 0, 1, jnp.where(power_two, coin_bits, 0)).astype(jnp.int32)


def level_of(stream_key, extent, split, least, high):
    def one(position, shards_of):
        heights = jax.random.uniform(jax.random.fold_in(jax.random.fold_in(stream_key, 6), position), (shards_of,), jnp.float32, least / len(split), high / len(split))
        return jnp.repeat(jnp.exp(heights), extent[position] // shards_of).reshape((-1,) + (1,) * (len(extent) - position - 1))

    gain = one(*split[0])
    for cut in split[1:]:
        gain = gain * one(*cut)
    return gain


def centred(stream_key, extent, scale, most, shards=(), dtype=jnp.bfloat16):
    entries = jax.random.normal(stream_key, extent, jnp.float32) * scale
    if len(shards) > 0:
        entries = level_of(stream_key, extent, shards, -0.22, 0.18) * entries
    return jnp.clip(entries, min=-most, max=most).astype(dtype)


def setup_inputs(seed: int = 0, part: int = 0) -> dict:
    key_of = jax.random.split(jax.random.key(seed), 7)
    part_keys = jax.random.split(jax.random.fold_in(key_of[6], part), 7)
    queries = draw_queries(jax.random.fold_in(jax.random.fold_in(key_of[6], part), 71), part)
    keys = draw_keys(jax.random.fold_in(jax.random.fold_in(key_of[6], part), 71), part)
    values = centred(part_keys[2], (TOKENS, CH), 1.0, 6.0, ((0, 32), (1, 4)))
    query_gain = jnp.clip(1.0 + 0.18 * jax.random.normal(key_of[3], (CH,), jnp.float32), 0.1, 1.9)
    key_gain = jnp.clip(1.0 + 0.18 * jax.random.normal(key_of[4], (CH,), jnp.float32), 0.1, 1.9)
    block_mask = draw_block_mask(jax.random.fold_in(key_of[6], 71), part)
    return dict(queries=queries, keys=keys, values=values, query_gain=query_gain, key_gain=key_gain, block_mask=block_mask)


def normalize(raw_rows, gain_vec):
    as_float = raw_rows.astype(jnp.float32)
    mean_square = lax.optimization_barrier(jnp.sum(as_float * as_float, axis=1, keepdims=True)) / (HEADS * HD)
    return (as_float * lax.rsqrt(mean_square + 1e-06) * gain_vec.astype(jnp.float32)[None, :]).astype(jnp.bfloat16)

def reference(queries, keys, values, query_gain, key_gain, block_mask):
    q_hat = normalize(queries, query_gain).reshape(TOKENS, HEADS, HD)
    k_float = normalize(keys, key_gain).reshape(TOKENS, HEADS, HD).astype(jnp.float32)
    v_float = values.reshape(TOKENS, HEADS, HD).astype(jnp.float32)
    key_block = (jnp.arange(TOKENS) // BLOCK).astype(jnp.int32)
    score_scale = HD ** (-0.5)

    def one_block(block_index):
        q_part = lax.dynamic_slice_in_dim(q_hat, (block_index * BLOCK).astype(jnp.int32), BLOCK, 0).astype(jnp.float32)
        mask_row = lax.dynamic_index_in_dim(block_mask, block_index.astype(jnp.int32), 0, keepdims=False)
        allowed = (mask_row[key_block] == 1)[None, None, :]
        scores = jnp.einsum('qhd,khd->hqk', q_part, k_float) * score_scale
        scores = jnp.where(allowed, scores, jnp.float32(-1e+30))
        row_max = lax.optimization_barrier(jnp.max(scores, axis=2, keepdims=True))
        weights = jnp.where(allowed, jnp.exp(scores - row_max), jnp.float32(0.0))
        weight_sum = lax.optimization_barrier(jnp.sum(weights, axis=2))
        rounded = lax.optimization_barrier(weights.astype(jnp.bfloat16))
        numer = jnp.einsum('hqk,khd->qhd', rounded.astype(jnp.float32), v_float)
        return (numer / weight_sum.T[:, :, None]).astype(jnp.bfloat16).reshape(BLOCK, HEADS * HD)
    blocks_out = lax.map(one_block, jnp.arange(NB).astype(jnp.int32))
    return blocks_out.reshape(TOKENS, HEADS * HD)
```

```python
import jax
import jax.numpy as jnp
from jax import lax
from jax.experimental import pallas as pl
from jax.experimental.pallas import tpu as pltpu
from jax.sharding import PartitionSpec as P

HEADS = 32
HD = 128
BLOCK = 128
ROW = 8
EXTRA = 16

epsilon = 1e-06
floor_score = -1e30
OFFSETS = (0, 1, -1, 2, -2, 4, -4, 8, -8)


def prep_kernel(q_ref, k_ref, v_ref, tot_ref, qg_ref, kg_ref, mask_ref, kv_ref, qm_ref):
    factor = lax.rsqrt(tot_ref[...] / (HEADS * HD) + epsilon)
    columns = jnp.transpose(factor)
    qf, kf = columns[:, 0:1], columns[:, 1:2]
    row = jnp.broadcast_to(mask_ref[...], (EXTRA, BLOCK)).astype(jnp.bfloat16)
    for h in range(ROW):
        cut = slice(h * HD, (h + 1) * HD)
        k = k_ref[:, cut].astype(jnp.float32) * kf * kg_ref[:, cut]
        kv_ref[h, :BLOCK, :] = k.astype(jnp.bfloat16)
        kv_ref[h, BLOCK:, :] = v_ref[:, cut]
        q = q_ref[:, cut].astype(jnp.float32) * qf * qg_ref[:, cut]
        qm_ref[h, :BLOCK, :] = q.astype(jnp.bfloat16)
        qm_ref[h, BLOCK:, :] = row


def attend_kernel(flag_ref, qm_ref, own_ref, prev_ref, next_ref, opp_ref, out_ref):
    rows = (prev_ref, own_ref, next_ref)
    for i in range(ROW):
        blocks = []
        for d in OFFSETS:
            j = ROW + i + d
            blocks.append((rows[j // ROW], j % ROW))
        blocks.append((opp_ref, i))
        q = qm_ref[i, :BLOCK, :]
        keys = jnp.concatenate([r[j, :BLOCK, :] for r, j in blocks], axis=0)
        scores = lax.dot_general(
            q, keys, (((1,), (1,)), ((), ())), preferred_element_type=jnp.float32
        ) * (HD ** (-0.5))
        parts = [
            jnp.where(flag_ref[i, n] > 0, scores[:, n * BLOCK : (n + 1) * BLOCK], floor_score)
            for n in range(len(blocks))
        ]
        top = parts[0]
        for part in parts[1:]:
            top = jnp.maximum(top, part)
        row_max = jnp.max(top, axis=1, keepdims=True)
        weights = [jnp.exp(part - row_max) for part in parts]
        total = weights[0]
        for w in weights[1:]:
            total = total + w
        weight_sum = jnp.sum(total, axis=1, keepdims=True)
        rounded = jnp.concatenate([w.astype(jnp.bfloat16) for w in weights], axis=1)
        vals = jnp.concatenate([r[j, BLOCK:, :] for r, j in blocks], axis=0)
        numer = jnp.dot(rounded, vals, preferred_element_type=jnp.float32)
        out_ref[i] = (numer / weight_sum).astype(jnp.bfloat16)


def local(queries, keys, values, query_gain, key_gain, block_mask):
    blocks = block_mask.shape[1]
    rows = blocks // ROW
    groups = [[z * ROW + y for y in range(ROW)] for z in range(rows)]
    z = lax.axis_index("ctx") // ROW

    sums = jnp.stack(
        [jnp.sum(jnp.square(a.astype(jnp.float32)), axis=1) for a in (queries, keys)]
    )
    totals = lax.psum(sums, "tp")
    totals = jnp.pad(totals, ((0, 6), (0, 0)))
    mask_row = jnp.pad(block_mask.astype(jnp.float32), ((0, 0), (0, BLOCK - blocks)))
    kv, qm = pl.pallas_call(
        prep_kernel,
        out_shape=(
            jax.ShapeDtypeStruct((ROW, 2 * BLOCK, HD), jnp.bfloat16),
            jax.ShapeDtypeStruct((ROW, BLOCK + EXTRA, HD), jnp.bfloat16),
        ),
        name="prep",
    )(queries, keys, values, totals, query_gain[None], key_gain[None], mask_row)

    kv = lax.all_to_all(kv, "ctx", 0, 0, axis_index_groups=groups)
    ids = range(blocks)
    ahead = [(c, c + ROW) for c in ids if c + ROW < blocks]
    back = [(c, c - ROW) for c in ids if c >= ROW]
    across = [(c, c ^ 16) for c in ids]
    kv_prev = lax.ppermute(kv, "ctx", ahead)
    kv_next = lax.ppermute(kv, "ctx", back)
    kv_opp = lax.ppermute(kv, "ctx", across)
    qm = lax.all_to_all(qm, "ctx", 0, 0, axis_index_groups=groups)

    centre = z * ROW + jnp.arange(ROW)
    wanted = jnp.stack([centre + d for d in OFFSETS] + [centre ^ 16], axis=1)
    mask_rows = qm[:, BLOCK, :blocks].astype(jnp.float32)
    picked = wanted[:, :, None] == jnp.arange(blocks)[None, None, :]
    flags = jnp.sum(jnp.where(picked, mask_rows[:, None, :], 0.0), axis=2).astype(jnp.int32)

    out = pl.pallas_call(
        attend_kernel,
        out_shape=jax.ShapeDtypeStruct((ROW, BLOCK, HD), jnp.bfloat16),
        in_specs=[pl.BlockSpec(memory_space=pltpu.SMEM)]
        + [pl.BlockSpec(memory_space=pltpu.VMEM)] * 5,
        name="attend",
    )(flags, qm, kv, kv_prev, kv_next, kv_opp)
    out = lax.all_to_all(out, "ctx", 0, 0, axis_index_groups=groups)
    return jnp.transpose(out, (1, 0, 2)).reshape(queries.shape)


def solution(mesh):
    in_specs = (
        P(("dp", "ctx"), "tp"),
        P(("dp", "ctx"), "tp"),
        P(("dp", "ctx"), "tp"),
        P("tp"),
        P("tp"),
        P("ctx", None),
    )
    out_specs = P(("dp", "ctx"), "tp")
    return jax.shard_map(local, mesh=mesh, in_specs=in_specs, out_specs=out_specs, check_vma=False)
```

```python
import jax
import jax.numpy as jnp
from jax import lax
from jax.experimental import pallas as pl
from jax.experimental.pallas import tpu as pltpu
from jax.sharding import PartitionSpec as P


HEADS = 32
HD = 128
BLOCK = 128
ROW = 8
EXTRA = 16

epsilon = 1e-06
floor_score = -1e30
OFFSETS = (0, 1, -1, 2, -2, 4, -4, 8, -8)
FAR = len(OFFSETS)


def prep_kernel(q_ref, k_ref, tot_ref, qg_ref, kg_ref, mask_ref, k_out, qm_out):
    totals = jnp.concatenate([tot_ref[...], jnp.zeros((6, BLOCK), jnp.float32)], axis=0)
    factor = lax.rsqrt(totals / (HEADS * HD) + epsilon)
    columns = jnp.transpose(factor)
    qf, kf = columns[:, 0:1], columns[:, 1:2]
    blocks = mask_ref.shape[1]
    row = jnp.broadcast_to(mask_ref[...].astype(jnp.float32), (EXTRA, blocks)).astype(jnp.bfloat16)
    for h in range(ROW):
        cut = slice(h * HD, (h + 1) * HD)
        k = k_ref[:, cut].astype(jnp.float32) * kf * kg_ref[:, cut]
        k_out[h] = k.astype(jnp.bfloat16)
        q = q_ref[:, cut].astype(jnp.float32) * qf * qg_ref[:, cut]
        qm_out[h, :BLOCK, :] = q.astype(jnp.bfloat16)
        qm_out[h, BLOCK:, :] = jnp.zeros((EXTRA, HD), jnp.bfloat16)
        qm_out[h, BLOCK:, :blocks] = row


def near_kernel(flag_ref, qm_ref, k_own, k_prev, k_next, v_own, v_prev, v_next, acc_ref, stat_ref):
    key_rows = (k_prev, k_own, k_next)
    value_rows = (v_prev, v_own, v_next)
    for i in range(ROW):
        spots = [((ROW + i + d) // ROW, (ROW + i + d) % ROW) for d in OFFSETS]
        q = qm_ref[i, :BLOCK, :]
        keys = jnp.concatenate([key_rows[r][j] for r, j in spots], axis=0)
        scores = lax.dot_general(
            q, keys, (((1,), (1,)), ((), ())), preferred_element_type=jnp.float32
        ) * (HD ** (-0.5))
        parts = [
            jnp.where(flag_ref[i, n] > 0, scores[:, n * BLOCK : (n + 1) * BLOCK], floor_score)
            for n in range(len(spots))
        ]
        top = parts[0]
        for part in parts[1:]:
            top = jnp.maximum(top, part)
        row_max = jnp.max(top, axis=1, keepdims=True)
        weights = [jnp.exp(part - row_max) for part in parts]
        total = weights[0]
        for w in weights[1:]:
            total = total + w
        weight_sum = jnp.sum(total, axis=1, keepdims=True)
        rounded = jnp.concatenate([w.astype(jnp.bfloat16) for w in weights], axis=1)
        vals = jnp.concatenate([value_rows[r][j] for r, j in spots], axis=0)
        acc_ref[i] = jnp.dot(rounded, vals, preferred_element_type=jnp.float32)
        half = (BLOCK, HD // 2)
        stat_ref[i] = jnp.concatenate(
            [jnp.broadcast_to(row_max, half), jnp.broadcast_to(weight_sum, half)], axis=1
        )


def far_kernel(flag_ref, qm_ref, k_far, v_far, acc_ref, stat_ref, out_ref):
    each = range(ROW)
    scores = [
        lax.dot_general(
            qm_ref[i, :BLOCK, :],
            k_far[i],
            (((1,), (1,)), ((), ())),
            preferred_element_type=jnp.float32,
        )
        * (HD ** (-0.5))
        for i in each
    ]
    scores = [jnp.where(flag_ref[i, FAR] > 0, scores[i], floor_score) for i in each]
    old_max = [stat_ref[i, :, 0:1] for i in each]
    tops = [jnp.max(scores[i], axis=1, keepdims=True) for i in each]
    new_max = [jnp.maximum(old_max[i], tops[i]) for i in each]
    weights = [jnp.exp(scores[i] - new_max[i]) for i in each]
    extra = [
        jnp.dot(weights[i].astype(jnp.bfloat16), v_far[i], preferred_element_type=jnp.float32)
        for i in each
    ]
    sums = [jnp.sum(weights[i], axis=1, keepdims=True) for i in each]
    shrink = [jnp.exp(old_max[i] - new_max[i]) for i in each]
    for i in each:
        total = stat_ref[i, :, HD // 2 : HD // 2 + 1] * shrink[i] + sums[i]
        numer = acc_ref[i] * shrink[i] + extra[i]
        out_ref[i] = (numer / total).astype(jnp.bfloat16)


def local(queries, keys, values, query_gain, key_gain, block_mask):
    tokens = queries.shape[0]
    blocks = block_mask.shape[1]
    rows = blocks // ROW
    groups = [[z * ROW + y for y in range(ROW)] for z in range(rows)]
    z = lax.axis_index("ctx") // ROW
    tile = jax.ShapeDtypeStruct((ROW, BLOCK, HD), jnp.bfloat16)
    wide = jax.ShapeDtypeStruct((ROW, BLOCK, HD), jnp.float32)

    def spread(x):
        return lax.all_to_all(x, "ctx", 0, 0, axis_index_groups=groups)

    def shift(x, step):
        pairs = [(c, (c + step * ROW) % blocks) for c in range(blocks)]
        return lax.ppermute(x, "ctx", pairs)

    v = jnp.transpose(values.reshape(tokens, ROW, HD), (1, 0, 2))
    v = spread(v)

    sums = jnp.stack(
        [jnp.sum(jnp.square(a.astype(jnp.float32)), axis=1) for a in (queries, keys)]
    )
    totals = lax.psum(sums, "tp")
    k, qm = pl.pallas_call(
        prep_kernel,
        out_shape=(tile, jax.ShapeDtypeStruct((ROW, BLOCK + EXTRA, HD), jnp.bfloat16)),
        name="prep",
    )(queries, keys, totals, query_gain[None], key_gain[None], block_mask)
    k = spread(k)

    v_prev = shift(v, 1)
    v_next = shift(v, -1)
    k_prev = shift(k, 1)
    k_next = shift(k, -1)
    qm = spread(qm)
    v_far = shift(v_prev, 1)
    k_far = shift(k_next, -1)

    centre = z * ROW + jnp.arange(ROW)
    wanted = jnp.stack([centre + d for d in OFFSETS] + [centre ^ 16], axis=1)
    mask_rows = qm[:, BLOCK, :blocks].astype(jnp.float32)
    picked = wanted[:, :, None] == jnp.arange(blocks)[None, None, :]
    flags = jnp.sum(jnp.where(picked, mask_rows[:, None, :], 0.0), axis=2).astype(jnp.int32)

    smem, vmem = pl.BlockSpec(memory_space=pltpu.SMEM), pl.BlockSpec(memory_space=pltpu.VMEM)
    cost = pl.CostEstimate(flops=600_000_000, bytes_accessed=4_000_000, transcendentals=1_200_000)
    acc, stat = pl.pallas_call(
        near_kernel,
        out_shape=(wide, wide),
        in_specs=[smem] + [vmem] * 7,
        cost_estimate=cost,
        name="near",
    )(flags, qm, k, k_prev, k_next, v, v_prev, v_next)
    out = pl.pallas_call(
        far_kernel,
        out_shape=tile,
        in_specs=[smem] + [vmem] * 5,
        name="far",
    )(flags, qm, k_far, v_far, acc, stat)
    out = spread(out)
    return jnp.transpose(out, (1, 0, 2)).reshape(queries.shape)


def solution(mesh):
    in_specs = (
        P(("dp", "ctx"), "tp"),
        P(("dp", "ctx"), "tp"),
        P(("dp", "ctx"), "tp"),
        P("tp"),
        P("tp"),
        P("ctx", None),
    )
    out_specs = P(("dp", "ctx"), "tp")

    return jax.shard_map(local, mesh=mesh, in_specs=in_specs, out_specs=out_specs, check_vma=False)
```
